32 devices in a mesh: wide: 8 (over z, x), narrow: 4 (over y, core).
Axes of the slice: x: 2, y: 2, z: 4, core: 2. Of those that a mesh axis runs over, the one named last changes fastest.
Arguments:
- potentials: float32 [8, 128, 128, 128], P('wide', 'narrow'), may hold values from -190 to 190
- parents: int32 [8], replicated, may hold values from 0 to 3, as said below
- separator_excluded: int32 [8], replicated, may hold values from 0 to 2
- measurement_clique: int32 [8], replicated, may hold values from 0 to 7, as said below
- measured: float32 [8, 128, 128], P('wide', 'narrow'), may hold values from 0.25 to 4
Outputs:
- marginal: float32 [8, 128, 128], P('wide', 'narrow')
- updated: float32 [8, 128, 128, 128], P('wide', 'narrow')
The draws below stay inside these ranges and needn't reach their ends.
Inputs may be any that keep to these rules, and one draw needn't show every extreme that they name: parents[0] = 0; a clique c with 1 <= c < 2 has parent 0, one with 2 <= c < 4 a parent in 1 to 1, and one with c >= 4 a parent in 2 to 3; the last clique has parent 4 - 1. `measurement_clique`: every clique is named by exactly one measured marginal.
All inputs are finite; a program needn't handle non-finite values.
Results may differ from the reference program's by a relative error of at most 0.0003.
Values sent between devices are 32-bit elements; how exact they have to be, the bound alone decides.
No kernel may reach another device: no remote copies, remote signals or barrier semaphores. Data moves between devices by JAX's collectives and lax.ppermute only.
A program may use at most 64 MiB of HBM per device.

```python
import math
import jax
import jax.numpy as jnp
from jax import lax

K = 128
DEPTH = 3
CLIQUE_COUNT = 8
LEVEL1 = 2
LEVEL2 = 4


def draw_parents(key, part):
    clique_numbers = jnp.arange(CLIQUE_COUNT, dtype=jnp.int32)
    lowest = jnp.where(clique_numbers < LEVEL1, 0, jnp.where(clique_numbers < LEVEL2, 1, LEVEL1)).astype(jnp.int32)
    beyond = jnp.where(clique_numbers < LEVEL1, 1, jnp.where(clique_numbers < LEVEL2, LEVEL1, LEVEL2)).astype(jnp.int32)
    raw_draw = jax.random.randint(key, (CLIQUE_COUNT,), 0, 1 << 20, dtype=jnp.int32)
    picked = (lowest + raw_draw % (beyond - lowest)).astype(jnp.int32)
    return jnp.where(clique_numbers == CLIQUE_COUNT - 1, LEVEL2 - 1, picked).astype(jnp.int32)


def draw_measurement_clique(key, part):
    count = CLIQUE_COUNT
    numbers = jnp.arange(count, dtype=jnp.int32)
    fixed_sources = jnp.array([count - 2, LEVEL2 + 1, (LEVEL2 + 1 + count // 2) % count], jnp.int32)
    fixed_targets = jnp.array([count - 1, LEVEL2, LEVEL2 + 1], jnp.int32)
    source_fixed = jnp.any(numbers[:, None] == fixed_sources[None, :], axis=1)
    target_fixed = jnp.any(numbers[:, None] == fixed_targets[None, :], axis=1)
    source_order = jnp.argsort(source_fixed.astype(jnp.int32) * count + numbers, stable=True).astype(jnp.int32)
    scores = jax.random.permutation(jax.random.fold_in(key, 11), count).astype(jnp.int32)
    target_order = jnp.argsort(target_fixed.astype(jnp.int32) * count + scores, stable=True).astype(jnp.int32)
    result = jnp.zeros((count,), jnp.int32).at[source_order].set(target_order)
    result = result.at[fixed_sources].set(fixed_targets)
    return result.astype(jnp.int32)


def draw_potentials(key, part):
    noise = jax.random.normal(key, (CLIQUE_COUNT, K, K, K), jnp.float32) * 1.5
    return jnp.clip(noise, -9.0, 9.0)


def with_ends(entries, rng, smallest, largest):
    place = [jax.random.randint(jax.random.fold_in(rng, axis), (), 0, length) for axis, length in enumerate(entries.shape)]
    longest = entries.shape.index(max(entries.shape))
    neighbour = place[:longest] + [(place[longest] + 1) % entries.shape[longest]] + place[longest + 1:]
    return entries.at[tuple(place)].set(smallest).at[tuple(neighbour)].set(largest)


def steps_of(stream_key, shape, shards, smallest, high):
    def one(axis_at, shards_of):
        steps = jax.random.uniform(jax.random.fold_in(jax.random.fold_in(stream_key, 6), axis_at), (shards_of,), jnp.float32, smallest / len(shards), high / len(shards))
        return jnp.repeat(jnp.exp(steps), shape[axis_at] // shards_of).reshape((-1,) + (1,) * (len(shape) - axis_at - 1))

    level = one(*shards[0])
    for cut in shards[1:]:
        level = level * one(*cut)
    return level


def setup_inputs(seed: int = 0) -> dict:
    streams_of = jax.random.split(jax.random.key(seed), 6)
    return {
        "potentials": draw_potentials(jax.random.fold_in(streams_of[5], 71), 0),
        "parents": draw_parents(jax.random.fold_in(streams_of[5], 71), 0),
        "separator_excluded": with_ends(jax.random.randint(streams_of[2], (CLIQUE_COUNT,), 0, 3), jax.random.fold_in(streams_of[2], 1), 0, 2).astype(jnp.int32),
        "measurement_clique": draw_measurement_clique(jax.random.fold_in(streams_of[5], 71), 0),
        "measured": jnp.clip(jnp.exp(math.log(4.0) - 2.7725887 * jax.random.uniform(streams_of[4], (CLIQUE_COUNT, K, K), jnp.float32) ** steps_of(streams_of[4], (CLIQUE_COUNT, K, K), ((0, 8), (1, 4)), -0.2, 0.2)), 0.25, 4.0),
    }


def log_sum(values, along):
    largest_entry = jnp.max(values, axis=along, keepdims=True)
    return jnp.squeeze(largest_entry, along) + jnp.log(jnp.sum(jnp.exp(values - largest_entry), axis=along))


def three_ways(table):
    return jnp.stack([log_sum(table, 0), log_sum(table, 1), log_sum(table, 2)])


def first_way(table):
    return log_sum(table, 0)


def reference(potentials, parents, separator_excluded, measurement_clique, measured):
    clique_numbers = jnp.arange(CLIQUE_COUNT, dtype=jnp.int32)
    belief = potentials
    for iteration in range(DEPTH):
        messages = lax.map(three_ways, belief)
        incoming = messages[parents, separator_excluded]
        incoming = jnp.where((clique_numbers > 0)[:, None, None], incoming, jnp.float32(0.0))
        belief = potentials + incoming[:, None, :, :]
    cell_lse = lax.map(first_way, belief)
    logz = log_sum(cell_lse.reshape(CLIQUE_COUNT, K * K), 1)
    marginal = jnp.float32(K * K) * jnp.exp(cell_lse - logz[:, None, None])
    sender_rows = jnp.zeros((CLIQUE_COUNT,), jnp.int32).at[measurement_clique].set(clique_numbers)
    residual = marginal - measured[sender_rows]
    is_leaf = (clique_numbers >= LEVEL2)[:, None, None]
    step_term = jnp.where(is_leaf, residual, jnp.float32(0.0))
    updated = potentials - jnp.float32(0.5) * step_term[:, None, :, :]
    return marginal, updated
```

```python
import functools

import jax
import jax.numpy as jnp
from jax import lax
from jax.experimental import pallas as pl
from jax.experimental.pallas import tpu as pltpu
from jax.sharding import PartitionSpec as P

DEPTH = 3
ABSENT = -1e30


def merged_2(part, axis, combine):
    gathered = jax.tree.map(lambda a: lax.all_gather(a, axis), part)

    def take(source):
        return jax.tree.map(lambda a: lax.dynamic_index_in_dim(a, source, 0, False), gathered)

    return lax.fori_loop(
        1, lax.axis_size(axis), lambda source, state: combine(state, take(source)), take(0)
    )


def log_sum(values, along):
    largest_entry = jnp.max(values, axis=along, keepdims=True)
    return jnp.squeeze(largest_entry, along) + jnp.log(
        jnp.sum(jnp.exp(values - largest_entry), axis=along)
    )


def join_tables(first, second):
    largest_entry = jnp.maximum(first[0], second[0])
    return (
        largest_entry,
        first[1] * jnp.exp(first[0] - largest_entry)
        + second[1] * jnp.exp(second[0] - largest_entry),
    )


def outgoing(belief, quarter_index, rows_here):
    largest_entry = jnp.max(belief, axis=0)
    summed = jnp.sum(jnp.exp(belief - largest_entry[None]), axis=0)
    merged = merged_2((largest_entry, summed), "narrow", join_tables)
    drop_first = merged[0] + jnp.log(merged[1])
    drop_first = lax.dynamic_slice_in_dim(drop_first, quarter_index * rows_here, rows_here, 0)
    return jnp.stack([drop_first, log_sum(belief, 1), log_sum(belief, 2)])


def route_rows(tables, parents, separator_excluded, self_index):
    kinds = jnp.arange(3, dtype=jnp.int32)
    chosen = (
        (separator_excluded[:, None] == kinds[None, :]) & (parents == self_index)[:, None]
    ).astype(jnp.float32)
    return jnp.einsum("ck,kqv->cqv", chosen, tables, precision=lax.Precision.HIGHEST)


def general_body(potentials, parents, separator_excluded, measurement_clique, measured):
    own_slab = potentials[0]
    rows_here = own_slab.shape[0]
    domain = own_slab.shape[2]
    self_index = lax.axis_index("wide")
    quarter_index = lax.axis_index("narrow")
    first_leaf = level_starts(lax.axis_size("wide"))[3]
    belief = own_slab
    for iteration in range(DEPTH):
        tables = outgoing(belief, quarter_index, rows_here)
        outbox = route_rows(tables, parents, separator_excluded, self_index)
        received = lax.all_to_all(outbox, "wide", split_axis=0, concat_axis=0, tiled=True)
        picked = jnp.sum(received, axis=0)
        complete = lax.all_gather(picked, "narrow", axis=0, tiled=True)
        complete = jnp.where(self_index > 0, complete, jnp.float32(0.0))
        belief = own_slab + complete[None]
    scale = jnp.float32(domain * domain)
    largest_entry = jnp.max(belief)
    summed = jnp.sum(jnp.exp(belief - largest_entry))
    merged = merged_2((largest_entry, summed), "narrow", join_tables)
    logz = merged[0] + jnp.log(merged[1])
    weighted = scale * jnp.sum(jnp.exp(belief - logz), axis=0)
    marginal = lax.psum_scatter(weighted, "narrow", scatter_dimension=0, tiled=True)
    source_row = jnp.sum(
        jnp.where(
            measurement_clique == self_index,
            jnp.arange(measurement_clique.shape[0], dtype=jnp.int32),
            0,
        )
    )
    pieces = lax.all_gather(measured, "wide", axis=0, tiled=True)
    row_ids = jnp.arange(pieces.shape[0], dtype=jnp.int32)
    selector = (row_ids == source_row).astype(jnp.float32)
    own_measure = jnp.einsum("m,mqk->qk", selector, pieces, precision=lax.Precision.HIGHEST)
    residual = marginal - own_measure
    residual_whole = lax.all_gather(residual, "narrow", axis=0, tiled=True)
    step_term = jnp.where(self_index >= first_leaf, residual_whole, jnp.float32(0.0))
    updated = own_slab - jnp.float32(0.5) * step_term[None]
    return (marginal[None], updated[None])


def level_starts(wide_count):
    first = 1 + max(1, wide_count // 16)
    return (0, 1, first, first + wide_count // 4, wide_count)


def move(x, wide_to, narrow_to):
    wide_count, narrow_count = lax.axis_size("wide"), lax.axis_size("narrow")
    pairs = [
        (w * narrow_count + q, (wide_to(w) % wide_count) * narrow_count + narrow_to(q) % narrow_count)
        for w in range(wide_count)
        for q in range(narrow_count)
    ]
    return lax.ppermute(x, ("wide", "narrow"), pairs)


def same(i):
    return i


def plus(k):
    return lambda i: i + k


def flip(k):
    return lambda i: i ^ k


def log_add(a, b):
    return jnp.maximum(a, b) + jnp.log(1.0 + jnp.exp(-jnp.abs(a - b)))


def in_vmem(x):
    return pltpu.with_memory_space_constraint(x, pltpu.VMEM)


def reduce_first(pot_ref, out_ref):
    domain = pot_ref.shape[1]

    def block(i, _):
        rows = pl.ds(pl.multiple_of(i * 8, 8), 8)
        x = pot_ref[:, rows, :]
        top = jnp.max(x, axis=0)
        out_ref[rows, :] = top + jnp.log(jnp.sum(jnp.exp(x - top[None]), axis=0))
        return 0

    lax.fori_loop(0, domain // 8, block, 0)


def reduce_later(kind, pot_ref, message_ref, top_ref, sum_ref):
    rows_here = pot_ref.shape[0]

    def group(i, _):
        for j in range(4):
            row = i * 4 + j
            t = pot_ref[row]
            if message_ref is not None:
                t = t + message_ref[...]
            if kind == 2:
                t = t.T
            top = jnp.max(t, axis=0, keepdims=True)
            top_ref[pl.ds(row, 1), :] = top
            sum_ref[pl.ds(row, 1), :] = jnp.sum(jnp.exp(t - top), axis=0, keepdims=True)
        return 0

    lax.fori_loop(0, rows_here // 4, group, 0)
    return top_ref[...] + jnp.log(sum_ref[...])


def own_rows(ref):
    rows = ref.shape[0] // lax.axis_size("narrow")
    return ref[pl.ds(pl.multiple_of(lax.axis_index("narrow") * rows, rows), rows), :]


def first_kernel(kind_ref, pot_ref, out_ref, top_ref, sum_ref):
    is_root = lax.axis_index("wide") == 0
    kind = kind_ref[1]
    rows = pot_ref.shape[0]
    mine = pl.ds(pl.multiple_of(lax.axis_index("narrow") * rows, rows), rows)

    @pl.when(jnp.logical_or(jnp.logical_not(is_root), kind == 0))
    def _():
        reduce_first(pot_ref, out_ref)

    for k in (1, 2):

        @pl.when(jnp.logical_and(is_root, kind == k))
        def _():
            out_ref[...] = jnp.full(out_ref.shape, ABSENT, jnp.float32)
            out_ref[mine, :] = reduce_later(k, pot_ref, None, top_ref, sum_ref)


def rest_kernel(kind_ref, pot_ref, first_ref, out_ref):
    again = jnp.logical_and(lax.axis_index("wide") == 0, kind_ref[1] != 0)

    @pl.when(again)
    def _():
        reduce_first(pot_ref, out_ref)

    @pl.when(jnp.logical_not(again))
    def _():
        out_ref[...] = first_ref[...]


def send_tiles(active, children, kind_ref, pot_ref, message_ref, whole_ref, tiles_ref, kept_ref, top_ref, sum_ref):
    def wants(k):
        return functools.reduce(jnp.logical_or, [kind_ref[c] == k for c in children])

    @pl.when(active)
    def _():
        kept_ref[0] = own_rows(whole_ref) + own_rows(message_ref)
        for k in (1, 2):

            @pl.when(wants(k))
            def _():
                kept_ref[k] = reduce_later(k, pot_ref, message_ref, top_ref, sum_ref)

        for slot, c in enumerate(children):
            tiles_ref[slot] = kept_ref[kind_ref[c]]


def second_kernel(kind_ref, pot_ref, one_ref, two_ref, whole_ref, mine_ref, tiles_ref, message_ref, kept_ref, top_ref, sum_ref):
    active = lax.axis_index("wide") == 1

    @pl.when(active)
    def _():
        message_ref[...] = log_add(one_ref[...], two_ref[...])
        mine_ref[...] = own_rows(message_ref)

    send_tiles(active, [3, 2], kind_ref, pot_ref, message_ref, whole_ref, tiles_ref, kept_ref, top_ref, sum_ref)


def third_kernel(kind_ref, pot_ref, one_ref, two_ref, whole_ref, mine_ref, tiles_ref, message_ref, kept_ref, top_ref, sum_ref):
    w = lax.axis_index("wide")
    q = lax.axis_index("narrow")
    rows = pot_ref.shape[0]
    active = jnp.logical_or(w == 2, w == 3)

    @pl.when(active)
    def _():
        for ref, receiver in ((one_ref, q), (two_ref, q ^ 1)):
            sender = (receiver + 3) & 3
            for slot, source in ((0, sender), (1, sender ^ 1)):
                message_ref[pl.ds(pl.multiple_of(source * rows, rows), rows), :] = ref[slot]
        mine_ref[...] = own_rows(message_ref)

    children = [(w + 2) & 7, (w + 4) & 7, ((w + 2) & 7) ^ 1, ((w + 4) & 7) ^ 1]
    send_tiles(active, children, kind_ref, pot_ref, message_ref, whole_ref, tiles_ref, kept_ref, top_ref, sum_ref)


def last_kernel(pot_ref, here_ref, there_ref, whole_ref, marginal_ref, updated_ref, term_ref, cells_ref, measure_ref):
    w = lax.axis_index("wide")
    q = lax.axis_index("narrow")
    rows = pot_ref.shape[0]
    domain = pot_ref.shape[2]

    @pl.when(pl.program_id(0) == 0)
    def _():
        for ref, base in ((here_ref, q), (there_ref, q ^ 1)):
            for slot, source in ((0, base), (1, base ^ 2)):
                span = pl.ds(pl.multiple_of(source * rows, rows), rows)
                cells_ref[span, :] = ref[slot] + whole_ref[span, :]
                measure_ref[span, :] = ref[slot + 2]
        cells = cells_ref[...]
        top = jnp.max(cells, axis=(0, 1), keepdims=True)
        logz = top + jnp.log(jnp.sum(jnp.exp(cells - top), axis=(0, 1), keepdims=True))
        marginal = jnp.float32(domain * domain) * jnp.exp(cells - logz)
        cells_ref[...] = marginal
        marginal_ref[...] = own_rows(cells_ref)
        is_leaf = w >= 4
        term_ref[...] = jnp.where(is_leaf, jnp.float32(0.5) * (marginal - measure_ref[...]), jnp.float32(0.0))

    step = updated_ref.shape[0]
    updated_ref[...] = pot_ref[pl.ds(pl.program_id(0) * step, step)] - term_ref[...][None]


def relay_body(potentials, parents, separator_excluded, measurement_clique, measured):
    rows, domain = potentials.shape[1], potentials.shape[3]
    me = lax.axis_index("wide")
    f32 = jnp.float32
    smem = pl.BlockSpec(memory_space=pltpu.SMEM)
    vmem = pl.BlockSpec(memory_space=pltpu.VMEM)
    table = jax.ShapeDtypeStruct((domain, domain), f32)
    tile = jax.ShapeDtypeStruct((rows, domain), f32)
    tile_scratch = pltpu.VMEM((rows, domain), f32)
    table_scratch = pltpu.VMEM((domain, domain), f32)

    pot = in_vmem(potentials[0])

    gathered = [measured[0]]
    ids = [me]
    for k in (4, 1):
        other = move(jnp.stack(gathered), flip(k), same)
        ids = ids + [i ^ k for i in ids]
        gathered = gathered + [other[i] for i in range(len(gathered))]

    def owned_by(c):
        return sum(jnp.where(measurement_clique[i] == c, g, f32(0.0)) for i, g in zip(ids, gathered))

    measure = owned_by(me) + move(owned_by(me ^ 2), flip(2), same)

    first = pl.pallas_call(
        first_kernel, out_shape=table, in_specs=[smem, vmem], out_specs=vmem,
        scratch_shapes=[tile_scratch, tile_scratch], name="first",
    )(separator_excluded, pot)
    chip = log_add(first, move(first, same, flip(1)))
    one = move(chip, plus(1), plus(1))
    two = move(one, same, flip(1))

    rest = pl.pallas_call(
        rest_kernel, out_shape=table, in_specs=[smem, vmem, vmem], out_specs=vmem, name="rest",
    )(separator_excluded, pot, first)
    whole = log_add(rest, move(rest, same, flip(1)))
    whole = log_add(whole, move(whole, same, flip(2)))

    scratch = [table_scratch, pltpu.VMEM((3, rows, domain), f32), tile_scratch, tile_scratch]

    def tiles(n):
        return jax.ShapeDtypeStruct((n, rows, domain), f32)

    mine_1, sent = pl.pallas_call(
        second_kernel, out_shape=(tile, tiles(2)), in_specs=[smem] + [vmem] * 4, out_specs=(vmem, vmem),
        scratch_shapes=scratch, name="second",
    )(separator_excluded, pot, one, two, whole)
    partner = move(sent, same, flip(1))
    from_a = move(jnp.stack([sent[0], partner[0]]), plus(2), plus(1))
    from_b = move(jnp.stack([sent[1], partner[1]]), lambda w: (w + 2) ^ 1, plus(1))
    one = jnp.where(me == 3, from_a, from_b)
    two = move(one, same, flip(1))

    mine_2, sent = pl.pallas_call(
        third_kernel, out_shape=(tile, tiles(4)), in_specs=[smem] + [vmem] * 4, out_specs=(vmem, vmem),
        scratch_shapes=scratch, name="third",
    )(separator_excluded, pot, one, two, whole)
    from_a = move(sent[:2], plus(2), same)
    from_b = move(sent[2:], lambda w: (w + 2) ^ 1, same)
    own_tile = jnp.where(parents[me] == me - 2, from_a[0], from_b[0])
    onward = jnp.where(parents[jnp.minimum(me + 2, 7)] == me - 2, from_a[1], from_b[1])
    relayed = move(onward, plus(2), same)
    relayed_across = move(onward, plus(2), flip(2))
    message = jnp.where(me >= 6, relayed, own_tile)
    message = jnp.where(me <= 3, mine_2, message)
    message = jnp.where(me <= 1, mine_1, message)
    message = jnp.where(me == 0, f32(0.0), message)
    across = move(jnp.stack([message, measure]), same, flip(2))
    here = jnp.stack([message, jnp.where(me >= 6, relayed_across, across[0]), measure, across[1]])
    there = move(here, same, flip(1))

    steps = 4
    once2 = lambda i: (0, 0)
    once3 = lambda i: (0, 0, 0)
    marginal, updated = pl.pallas_call(
        last_kernel,
        grid=(steps,),
        out_shape=(tile, jax.ShapeDtypeStruct((rows, domain, domain), f32)),
        in_specs=[vmem, vmem, vmem, vmem],
        out_specs=(
            pl.BlockSpec((rows, domain), once2),
            pl.BlockSpec((rows // steps, domain, domain), lambda i: (i, 0, 0)),
        ),
        scratch_shapes=[table_scratch, table_scratch, table_scratch],
        name="last",
    )(pot, here, there, whole)
    return (marginal[None], updated[None])


def solution(mesh):
    wide_count, narrow_count = mesh.shape["wide"], mesh.shape["narrow"]
    starts = level_starts(wide_count)
    widths = tuple(b - a for a, b in zip(starts, starts[1:]))
    relay = widths == (1, 1, 2, 4) and narrow_count == 4
    return jax.shard_map(
        relay_body if relay else general_body,
        mesh=mesh,
        in_specs=(P("wide", "narrow", None, None), P(), P(), P(), P("wide", "narrow", None)),
        out_specs=(P("wide", "narrow", None), P("wide", "narrow", None, None)),
        check_vma=False,
    )
```
